128 devices in a mesh: pole: 2 (over y_lo), wave: 64 (over z, x, y_hi, core).
Axes of the slice: x: 4, y: 4 (y_hi: 2, y_lo: 2; y = y_hi * 2 + y_lo), z: 4, core: 2. Of those that a mesh axis runs over, the one named last changes fastest.
Arguments:
- tendency: bfloat16 [6, 2560, 128, 128], P('pole', 'wave'), may hold values from -6 to 6
- spectral_state: bfloat16 [6, 128, 128, 1280], P('pole', 'wave'), may hold values from -6 to 6
- legendre: bfloat16 [128, 1280, 2560], P('wave'), may hold values from -0.15625 to 0.15625
- gauss_weights: float32 [2560], P('wave'), may hold values from 0.35 to 1.05
- block_inverses: bfloat16 [64, 18, 128, 1280], P('pole', None, 'wave'), may hold values from -0.21875 to 0.21875
- pole_coeffs: float32 [64, 2], P('pole'), may hold values from -4 to 4
- wavenumbers: int32 [128], P('wave'), may hold values from 0 to 1279, as said below
Outputs:
- grid_state: bfloat16 [6, 2560, 128, 128], P('pole', 'wave')
The draws below stay inside these ranges and needn't reach their ends.
Inputs may be any that keep to these rules, and one draw needn't show every extreme that they name: `wavenumbers`: entries 2 i and 2 i + 1 hold w and 1279 - w for some w below 640; all entries differ, and 0 is among them.
All inputs are finite; a program needn't handle non-finite values.
Results may differ from the reference program's by a relative error of at most 0.0062.
Values may be sent and summed in bfloat16 or wider, within the bound.
A program may use at most 128 MiB of HBM per device.

```python
import jax
import jax.numpy as jnp
from jax import lax

NSPEC = 1280
NLAT = 2560
PAIRS = 64
MEMBERS = 128
M = 128


def draw_wavenumbers(key, part):
    halfway = NSPEC // 2
    device_count = M // 2
    shuffled = jax.random.permutation(jax.random.fold_in(key, 11), halfway - 1) + 1
    chosen = jnp.concatenate([jnp.zeros((1,), jnp.int32), shuffled[:device_count - 1].astype(jnp.int32)])
    chosen = jax.random.permutation(jax.random.fold_in(key, 12), chosen)
    paired = jnp.stack([chosen, NSPEC - 1 - chosen], axis=1)
    return paired.reshape(-1).astype(jnp.int32)


def shard_levels(key, dims, pieces, low, high):
    def one(position, blocks):
        heights = jax.random.uniform(jax.random.fold_in(jax.random.fold_in(key, 6), position), (blocks,), jnp.float32, low / len(pieces), high / len(pieces))
        return jnp.repeat(jnp.exp(heights), dims[position] // blocks).reshape((-1,) + (1,) * (len(dims) - position - 1))

    loudness = one(*pieces[0])
    for cut in pieces[1:]:
        loudness = loudness * one(*cut)
    return loudness


def scatter_about(stream_key, dims, spread, most, cuts=(), kind=jnp.bfloat16):
    entries = jax.random.normal(stream_key, dims, jnp.float32) * spread
    if len(cuts) > 0:
        entries = shard_levels(stream_key, dims, cuts, -0.22, 0.18) * entries
    return jnp.clip(entries, min=-most, max=most).astype(kind)


def setup_inputs(seed: int = 0) -> dict:
    keys = jax.random.split(jax.random.key(seed), 8)
    return {
        "tendency": scatter_about(keys[0], (6, NLAT, M, MEMBERS), 1.0, 6.0, ((0, 2), (1, 64))),
        "spectral_state": scatter_about(keys[1], (6, M, MEMBERS, NSPEC), 1.0, 6.0, ((0, 2), (1, 64))),
        "legendre": scatter_about(keys[2], (M, NSPEC, NLAT), NSPEC ** -0.5, 0.15625, ((0, 64),)),
        "gauss_weights": jnp.clip(0.35 + 0.699999958 * jax.random.uniform(keys[3], (NLAT,), jnp.float32) ** shard_levels(keys[3], (NLAT,), ((0, 64),), -0.2, 0.2), 0.35, 1.05),
        "block_inverses": scatter_about(keys[4], (PAIRS, 18, M, NSPEC), (PAIRS * 12) ** -0.5, 0.21875, ((0, 2), (2, 64))),
        "pole_coeffs": scatter_about(keys[5], (PAIRS, 2), 1.0, 4.0, ((0, 2),), jnp.float32),
        "wavenumbers": draw_wavenumbers(jax.random.fold_in(keys[7], 71), 0),
    }


def mix_rows(real_matrix, imag_matrix, leading, trailing, orientation):
    summed = jnp.zeros(leading.shape, jnp.float32)
    for column in range(3):
        summed = summed + real_matrix[:, column, :, None, :] * leading[column][None]
        summed = summed + orientation * imag_matrix[:, column, :, None, :] * trailing[column][None]
    return summed


def reference(tendency, spectral_state, legendre, gauss_weights, block_inverses, pole_coeffs, wavenumbers):
    weighted = (tendency.astype(jnp.float32) * gauss_weights[None, :, None, None]).astype(jnp.bfloat16)

    def analyse(slot_index):
        grid_slot = lax.dynamic_index_in_dim(weighted, slot_index, 2, keepdims=False).astype(jnp.float32)
        legendre_slot = lax.dynamic_index_in_dim(legendre, slot_index, 0, keepdims=False).astype(jnp.float32)
        return jnp.einsum('rje,nj->ren', grid_slot, legendre_slot)

    spectral_tend = jnp.transpose(lax.map(analyse, jnp.arange(M, dtype=jnp.int32)), (1, 0, 2, 3))
    degree = jnp.arange(NSPEC, dtype=jnp.int32)
    live_mask = (degree[None, :] >= wavenumbers[:, None]).astype(jnp.float32)
    forced = ((spectral_state.astype(jnp.float32) + spectral_tend) * live_mask[None, :, None, :]).astype(jnp.bfloat16)

    def add_pair(summed, pair_data):
        inverse, coefficient = pair_data
        inverse = inverse.astype(jnp.float32).reshape(2, 3, 3, M, NSPEC)
        real_part = coefficient[0] * inverse[0] - coefficient[1] * inverse[1]
        imag_part = coefficient[0] * inverse[1] + coefficient[1] * inverse[0]
        return (summed[0] + real_part, summed[1] + imag_part), None

    zeros_matrix = jnp.zeros((3, 3, M, NSPEC), jnp.float32)
    matrices, unused = lax.scan(add_pair, (zeros_matrix, zeros_matrix), (block_inverses, pole_coeffs))
    real_matrix, imag_matrix = matrices
    forced_wide = forced.astype(jnp.float32)
    real_rows = mix_rows(real_matrix, imag_matrix, forced_wide[:3], forced_wide[3:], -1.0)
    imag_rows = mix_rows(real_matrix, imag_matrix, forced_wide[3:], forced_wide[:3], 1.0)
    advanced = jnp.concatenate([real_rows, imag_rows], axis=0).astype(jnp.bfloat16)

    def synthesise(slot_index):
        spectra = lax.dynamic_index_in_dim(advanced, slot_index, 1, keepdims=False).astype(jnp.float32)
        legendre_slot = lax.dynamic_index_in_dim(legendre, slot_index, 0, keepdims=False).astype(jnp.float32)
        return jnp.einsum('ren,nj->rje', spectra, legendre_slot)

    synthesized = lax.map(synthesise, jnp.arange(M, dtype=jnp.int32))
    return jnp.transpose(synthesized, (1, 2, 0, 3)).astype(jnp.bfloat16)
```

```python
import jax
import jax.numpy as jnp
from jax import lax
from jax.sharding import PartitionSpec as P

SWAP = [(0, 1), (1, 0)]
EVERY = ("pole", "wave")


def per_device(
    tendency, spectral_state, legendre, gauss_weights, block_inverses, pole_coeffs, wavenumbers
):
    rows, lats, slots, members = tendency.shape
    waves = slots // 2
    degrees = legendre.shape[1]
    pole = lax.axis_index("pole")
    weighted = (tendency.astype(jnp.float32) * gauss_weights[None, :, None, None]).astype(
        jnp.bfloat16
    )
    outgoing = weighted.reshape(rows, lats, waves, 2, members).transpose(3, 2, 0, 1, 4)
    outgoing = outgoing.reshape(2 * waves, rows, lats, members)
    received = lax.all_to_all(outgoing, EVERY, split_axis=0, concat_axis=0, tiled=True)
    received = received.reshape(2, waves, rows, lats, members).transpose(0, 2, 1, 3, 4)
    received = received.reshape(2 * rows, waves * lats, members)

    own_state = lax.dynamic_index_in_dim(spectral_state, pole, 1, keepdims=False)
    other_state = lax.dynamic_index_in_dim(spectral_state, 1 - pole, 1, keepdims=False)
    other_state = lax.ppermute(other_state, "pole", SWAP)
    state = jnp.where(
        pole == 0,
        jnp.concatenate([own_state, other_state], 0),
        jnp.concatenate([other_state, own_state], 0),
    )

    local_pairs = block_inverses.shape[0]
    flat_inverse = block_inverses.reshape(local_pairs, -1).astype(jnp.float32)
    sums = jnp.dot(pole_coeffs.T, flat_inverse, precision=lax.Precision.HIGHEST)
    sums = sums.reshape(2, 2, 3, 3, 2, degrees)
    matrices = jnp.stack([sums[0, 0] - sums[1, 1], sums[0, 1] + sums[1, 0]])
    own_sum = lax.dynamic_index_in_dim(matrices, pole, 3, keepdims=False)
    other_sum = lax.dynamic_index_in_dim(matrices, 1 - pole, 3, keepdims=False)
    matrices = own_sum + lax.ppermute(other_sum, "pole", SWAP)
    real_matrix, imag_matrix = matrices[0], matrices[1]

    table = lax.dynamic_index_in_dim(legendre, pole, 0, keepdims=False)
    wavenumber = lax.dynamic_index_in_dim(wavenumbers, pole, 0, keepdims=False)
    tend = jnp.einsum("rje,nj->ren", received, table, preferred_element_type=jnp.float32)
    live = (lax.broadcasted_iota(jnp.int32, (1, 1, degrees), 2) >= wavenumber).astype(jnp.float32)
    forced = ((state.astype(jnp.float32) + tend) * live).astype(jnp.bfloat16)
    wide = forced.astype(jnp.float32)
    real_rows, imag_rows = [], []
    for row in range(3):
        real = jnp.zeros(wide.shape[1:], jnp.float32)
        imag = jnp.zeros(wide.shape[1:], jnp.float32)
        for column in range(3):
            re, im = real_matrix[row, column][None], imag_matrix[row, column][None]
            real = real + re * wide[column] - im * wide[3 + column]
            imag = imag + re * wide[3 + column] + im * wide[column]
        real_rows.append(real)
        imag_rows.append(imag)
    advanced = jnp.stack(real_rows + imag_rows).astype(jnp.bfloat16)
    grid = jnp.einsum(
        "ren,nj->rje", advanced, table, preferred_element_type=jnp.float32
    ).astype(jnp.bfloat16)
    grid = grid.reshape(2, rows, waves, lats, members).transpose(0, 2, 1, 3, 4)
    grid = grid.reshape(2 * waves, rows, lats, members)
    back = lax.all_to_all(grid, EVERY, split_axis=0, concat_axis=0, tiled=True)
    back = back.reshape(2, waves, rows, lats, members).transpose(2, 3, 1, 0, 4)
    return back.reshape(rows, lats, slots, members)


def solution(mesh):
    in_specs = (
        P("pole", "wave", None, None),
        P("pole", "wave", None, None),
        P("wave", None, None),
        P("wave"),
        P("pole", None, "wave", None),
        P("pole", None),
        P("wave"),
    )
    return jax.shard_map(
        per_device,
        mesh=mesh,
        in_specs=in_specs,
        out_specs=P("pole", "wave", None, None),
        check_vma=False,
    )
```
